32 devices in a mesh: segment: 4 (over z), ctx: 4 (over y, x), tp: 2 (over core).
Axes of the slice: x: 2, y: 2, z: 4, core: 2. Of those that a mesh axis runs over, the one named last changes fastest.
Arguments:
- queries: bfloat16 [4, 512, 8, 640], P('segment', 'ctx', 'tp'), may hold values from -200 to 200
- pairs: bfloat16 [4, 512, 8, 256], P('segment', 'ctx', 'tp'), may hold values from -6 to 6
- out_proj: bfloat16 [4, 8, 640, 5120], P('segment', 'tp'), may hold values from -0.625 to 0.625
- lengths: int32 [4, 4], replicated, may hold values from 1 to 256, 512 in all within a row
Outputs:
- scored: bfloat16 [4, 512, 5120], P('segment', 'ctx', 'tp')
The draws below stay inside these ranges and needn't reach their ends.
Inputs may be any that keep to these rules, and one draw needn't show every extreme that they name: `lengths`: each row sums to 512; its largest length is exactly 256.
All inputs are finite; a program needn't handle non-finite values.
Results may differ from the reference program's by a relative error of at most 0.014.
Values may be sent and summed in bfloat16 or wider, within the bound.
A program may use at most 64 MiB of HBM per device.

```python
import math
import jax
import jax.numpy as jnp
import numpy as np
from jax import lax

D = 5120
HEADS = 40
KVH = 8
HD = 128
ROLLS = 4
GROUP = 5
SEQ = 512
MBATCH = 4
N_TP = 2


def base_draw(key):
    shape = (MBATCH, SEQ, KVH, HD)
    key_part = jnp.clip(jax.random.normal(jax.random.fold_in(key, 101), shape, jnp.float32), -6.0, 6.0)
    value_part = jnp.clip(jax.random.normal(jax.random.fold_in(key, 102), shape, jnp.float32), -6.0, 6.0)
    query_part = jnp.clip(jax.random.normal(jax.random.fold_in(key, 103), (MBATCH, SEQ, KVH, GROUP, HD), jnp.float32), -6.0, 6.0)
    return (query_part, key_part, value_part)


def draw_queries(key, part):
    query_part, key_part, value_part = base_draw(key)
    return query_part.reshape(MBATCH, SEQ, KVH, GROUP * HD).astype(jnp.bfloat16)


def draw_pairs(key, part):
    query_part, key_part, value_part = base_draw(key)
    return jnp.concatenate([key_part, value_part], axis=3).astype(jnp.bfloat16)


def levels(own_key, extent, pieces, low, high):
    factor_of = 1.0
    for position, shards_of in pieces:
        steps = jax.random.uniform(jax.random.fold_in(jax.random.fold_in(own_key, 6), position), (shards_of,), jnp.float32, low / len(pieces), high / len(pieces))
        factor_of = factor_of * jnp.repeat(jnp.exp(steps), extent[position] // shards_of).reshape((-1,) + (1,) * (len(extent) - 1 - position))
    return factor_of


def profile(number_of, total, reach, skew):
    loads = [(1 << 20) // math.isqrt(standing ** skew) + 1 for standing in range(2, number_of + 1)]
    surplus, counts = total - reach - (number_of - 1), [1] * (number_of - 1)
    while surplus > 0:
        candidates = [i for i in range(number_of - 1) if counts[i] < reach]
        pool, left = sum([loads[i] for i in candidates]), surplus
        for i in candidates:
            extra = min(reach - counts[i], max(1, left * loads[i] // pool), surplus)
            counts[i] = counts[i] + extra
            surplus = surplus - extra
    return np.array([reach] + counts)


def ragged(rng, number_of, total, bound, skew):
    if number_of == 2:
        one = jax.random.randint(rng, (), max(1, total - bound), min(bound, total - 1) + 1)
        return jnp.stack([one, total - one])
    sizes = jnp.asarray(profile(number_of, total, bound, skew), jnp.int32)
    twos = (number_of - 1) // 2
    donor, sink = sizes[1:1 + 2 * twos:2], sizes[2:2 + 2 * twos:2]
    margin = jnp.minimum(donor - 1, bound - sink)
    moved = jax.random.randint(jax.random.fold_in(rng, 1), (twos,), 0, 1 << 20) % (margin + 1)
    sizes = sizes.at[1:1 + 2 * twos:2].set(donor - moved).at[2:2 + 2 * twos:2].set(sink + moved)
    return sizes[jax.random.permutation(jax.random.fold_in(rng, 2), number_of)]


def gaussian(rng, extent, scale, most, cuts=(), kind=jnp.bfloat16):
    factor_of = levels(rng, extent, cuts, -0.22, 0.18) if cuts else 1.0
    entries = jax.random.normal(rng, extent, jnp.float32) * scale * factor_of
    return jnp.minimum(jnp.maximum(entries, -most), most).astype(kind)


def setup_inputs(seed: int = 0) -> dict:
    key_list = jax.random.split(jax.random.key(seed), 5)
    queries = draw_queries(jax.random.fold_in(key_list[4], 71), 0)
    pairs = draw_pairs(jax.random.fold_in(key_list[4], 71), 0)
    out_proj = gaussian(key_list[2], (MBATCH, KVH, GROUP * HD, D), (HEADS * HD // 64) ** -0.5, 0.625, ((0, 4), (1, 2)))
    lengths = jax.vmap(lambda own: ragged(own, ROLLS, SEQ, SEQ // 2, 2))(jax.random.split(key_list[3], MBATCH)).reshape((MBATCH, ROLLS)).astype(jnp.int32)
    return dict(queries=queries, pairs=pairs, out_proj=out_proj, lengths=lengths)


def rollout_ids(positions, row_lengths):
    row_ends = jnp.cumsum(row_lengths).astype(jnp.int32)
    return lax.optimization_barrier(jnp.sum((positions[:, None] >= row_ends[None, :]).astype(jnp.int32), axis=1)).astype(jnp.int32)

def attend_batch(query_rows, pair_rows, row_lengths):
    seq_len = query_rows.shape[0]
    head_dim = pair_rows.shape[2] // 2
    kv_heads = pair_rows.shape[1]
    group_size = query_rows.shape[2] // head_dim
    block_rows = math.gcd(seq_len, 512)
    positions = jnp.arange(seq_len, dtype=jnp.int32)
    rollout = rollout_ids(positions, row_lengths)
    key_rows = pair_rows[:, :, :head_dim].astype(jnp.float32)
    value_rows = pair_rows[:, :, head_dim:].astype(jnp.float32)
    score_scale = 1.0 / math.sqrt(head_dim)

    def one_block(block_index):
        begin = (block_index * block_rows).astype(jnp.int32)
        query_block = lax.dynamic_slice_in_dim(query_rows, begin, block_rows, 0)
        query_block = query_block.astype(jnp.float32).reshape(block_rows, kv_heads, group_size, head_dim)
        row_pos = begin + jnp.arange(block_rows, dtype=jnp.int32)
        row_rollout = lax.dynamic_slice_in_dim(rollout, begin, block_rows, 0)
        scores = jnp.einsum('rhgd,khd->hgrk', query_block, key_rows) * score_scale
        visible = (row_rollout[:, None] == rollout[None, :]) & (positions[None, :] <= row_pos[:, None])
        scores = jnp.where(visible, scores, -1e+30)
        row_peak = lax.optimization_barrier(jnp.max(scores, axis=-1, keepdims=True))
        weights = jnp.where(visible, jnp.exp(scores - row_peak), 0.0)
        denom = lax.optimization_barrier(jnp.sum(weights, axis=-1))
        probs = lax.optimization_barrier(weights.astype(jnp.bfloat16)).astype(jnp.float32)
        outputs = jnp.einsum('hgrk,khd->hgrd', probs, value_rows) / denom[..., None]
        return jnp.transpose(outputs, (2, 0, 1, 3)).reshape(block_rows, kv_heads, group_size * head_dim)
    blocks = lax.map(one_block, jnp.arange(seq_len // block_rows, dtype=jnp.int32))
    return blocks.reshape(seq_len, kv_heads, group_size * head_dim).astype(jnp.bfloat16)

def reference(queries, pairs, out_proj, lengths):

    def one_section(section):
        batch_index = ((section + 1) % MBATCH).astype(jnp.int32)
        attended = attend_batch(queries[batch_index], pairs[batch_index], lengths[batch_index])
        head_parts = attended.reshape(SEQ, N_TP, -1)
        weight_parts = out_proj[section].reshape(N_TP, -1, D)
        summed = jnp.zeros((SEQ, D), jnp.float32)
        for group_index in range(N_TP):
            partial_sum = jnp.dot(head_parts[:, group_index], weight_parts[group_index], preferred_element_type=jnp.float32)
            summed = summed + lax.optimization_barrier(partial_sum.astype(jnp.bfloat16)).astype(jnp.float32)
        return summed.astype(jnp.bfloat16)
    return lax.map(one_section, jnp.arange(MBATCH, dtype=jnp.int32))
```

```python
import functools
import math

import jax
import jax.numpy as jnp
from jax import lax
from jax.experimental import pallas as pl
from jax.experimental.layout import Layout, with_layout_constraint
from jax.experimental.pallas import tpu as pltpu
from jax.sharding import PartitionSpec as P

MESH = pl.DeviceIdType.MESH
HIDDEN = -1e30


def tile_of(columns):
    for tile in (1280, 640, 512, 256, 128):
        if columns % tile == 0:
            return tile
    return columns


def kernel(
    sizes,
    lengths_hbm,
    q_hbm,
    kv_hbm,
    w_hbm,
    out_ref,
    lengths_ref,
    q_raw,
    kv_raw,
    q_wide,
    kv_wide,
    q_ref,
    kv_ref,
    ship_q,
    ship_kv,
    w_ref,
    last_w,
    seen_ref,
    hide_ref,
    sent_ref,
    got_ref,
    peer_got,
    acc_ref,
    part_ref,
    share_ref,
    lengths_sem,
    raw_sem,
    w_sem,
    own_w_sem,
    peer_w_send,
    peer_w_recv,
    ship_send,
    ship_recv,
    seen_send,
    seen_recv,
    att_send,
    att_recv,
    fwd_send,
    fwd_recv,
    share_send,
    share_recv,
):
    n_seg, n_ctx, n_tp, rows, heads, head_dim, group, back, shipped = sizes
    seg = lax.axis_index("segment")
    ctx = lax.axis_index("ctx")
    tp = lax.axis_index("tp")
    width = group * head_dim
    columns = out_ref.shape[1]
    tile = tile_of(columns)
    tiles = columns // tile
    depth = (back + 1) * rows
    own = heads - shipped
    last = own - 1
    early = [h for h in range(heads) if h != last]
    to_seg = lax.rem(seg + n_seg - 1, n_seg)
    from_seg = lax.rem(seg + 1, n_seg)
    relays = n_ctx == 4 and back == 2

    def relayed(h):
        return relays and h > 0

    lengths_copy = pltpu.make_async_copy(lengths_hbm, lengths_ref, lengths_sem)
    kv_copy = pltpu.make_async_copy(kv_hbm, kv_raw, raw_sem.at[0])
    q_copy = pltpu.make_async_copy(q_hbm, q_raw, raw_sem.at[1])
    kv_copy.start()
    q_copy.start()
    lengths_copy.start()

    barrier = pltpu.get_barrier_semaphore()

    def sends_to(source, by, h=0):
        there = (source >= 0) & (source + by < n_ctx)
        return there & (source != 1) if relayed(h) and by == 1 else there

    awaited = jnp.int32(1 + n_tp - 1)
    pl.semaphore_signal(
        barrier, inc=1, device_id={"segment": from_seg}, device_id_type=MESH
    )
    for by in range(1, back + 1):
        awaited = awaited + sends_to(ctx, by).astype(jnp.int32)

        @pl.when(sends_to(ctx - by, by))
        def _():
            pl.semaphore_signal(
                barrier, inc=1, device_id={"ctx": ctx - by}, device_id_type=MESH
            )

    if relays:
        awaited = awaited + (ctx == 3).astype(jnp.int32)

        @pl.when(ctx == 2)
        def _():
            pl.semaphore_signal(
                barrier, inc=1, device_id={"ctx": 3}, device_id_type=MESH
            )

    for by in range(1, n_tp):
        pl.semaphore_signal(
            barrier,
            inc=1,
            device_id={"tp": lax.rem(tp + by, n_tp)},
            device_id_type=MESH,
        )

    def w_copy(n):
        return pltpu.make_async_copy(
            w_hbm.at[pl.ds(early[n] * width, width)],
            w_ref.at[pl.ds(n * width, width)],
            w_sem.at[n],
        )

    def own_w_copy(g):
        return pltpu.make_async_copy(
            w_hbm.at[
                pl.ds(last * width + g * head_dim, head_dim),
                pl.ds(pl.multiple_of(tp * columns, columns), columns),
            ],
            last_w.at[g, pl.ds(0, head_dim)],
            own_w_sem.at[g],
        )

    def peer_w_copy(by, g):
        peer = lax.rem(tp + by, n_tp)
        return pltpu.make_async_remote_copy(
            src_ref=w_hbm.at[
                pl.ds(last * width + g * head_dim, head_dim),
                pl.ds(pl.multiple_of(peer * columns, columns), columns),
            ],
            dst_ref=last_w.at[g, pl.ds(by * head_dim, head_dim)],
            send_sem=peer_w_send.at[by - 1, g],
            recv_sem=peer_w_recv.at[by - 1, g],
            device_id={"tp": peer},
            device_id_type=MESH,
        )

    def split_kv(h, ref):
        for part in range(2):
            ref[:, part * head_dim : (part + 1) * head_dim] = kv_wide[
                pl.ds(part * heads + h, rows, stride=2 * heads), :
            ].astype(jnp.bfloat16)

    def split_q(h, ref, base):
        for g in range(group):
            ref[base + g] = q_wide[
                pl.ds(g * heads + h, rows, stride=group * heads), :
            ].astype(jnp.bfloat16)

    kv_copy.wait()
    kv_wide[...] = kv_raw[...].astype(jnp.float32)
    for h in range(own):
        split_kv(h, kv_ref.at[h])
    if shipped:
        split_kv(own, ship_kv)
    q_copy.wait()
    q_wide[...] = q_raw[...].astype(jnp.float32)
    if shipped:
        split_q(own, ship_q, 0)

    pl.semaphore_wait(barrier, awaited)

    def ship(n):
        return pltpu.make_async_remote_copy(
            src_ref=(ship_kv, ship_q)[n],
            dst_ref=(kv_ref.at[own], q_ref.at[pl.ds(own * group, group)])[n],
            send_sem=ship_send.at[n],
            recv_sem=ship_recv.at[n],
            device_id={"segment": to_seg},
            device_id_type=MESH,
        )

    def kv_send(by, h):
        return pltpu.make_async_remote_copy(
            src_ref=kv_ref.at[h],
            dst_ref=seen_ref.at[h, by - 1],
            send_sem=seen_send.at[by - 1, h],
            recv_sem=seen_recv.at[by - 1, h],
            device_id={"ctx": lax.rem(ctx + by, n_ctx)},
            device_id_type=MESH,
        )

    def relay(h):
        return pltpu.make_async_remote_copy(
            src_ref=seen_ref.at[h, 1],
            dst_ref=seen_ref.at[h, 0],
            send_sem=seen_send.at[0, h],
            recv_sem=seen_recv.at[0, h],
            device_id={"ctx": 2},
            device_id_type=MESH,
        )

    def spread(h):
        for by in range(back, 0, -1):

            @pl.when(sends_to(ctx, by, h))
            def _():
                kv_send(by, h).start()

    if shipped:
        for n in range(2):
            ship(n).start()
    for h in range(own):
        spread(h)
    for n in range(len(early)):
        w_copy(n).start()
    for g in range(group):
        own_w_copy(g).start()
        for by in range(1, n_tp):
            peer_w_copy(by, g).start()

    for by in range(1, back + 1):

        @pl.when(ctx < by)
        def _():
            for h in range(heads):
                seen_ref[h, by - 1] = jnp.zeros((rows, 2 * head_dim), seen_ref.dtype)

    for h in range(own):
        split_q(h, q_ref, h * group)

    lengths_copy.wait()
    query_pos = ctx * rows + lax.broadcasted_iota(jnp.int32, (rows, depth), 0)
    key_pos = (ctx - back) * rows + lax.broadcasted_iota(jnp.int32, (rows, depth), 1)

    def hide(n, batch):
        first = jnp.zeros((rows, depth), jnp.int32)
        end = jnp.int32(0)
        for k in range(lengths_ref.shape[1]):
            end = end + lengths_ref[batch, k]
            first = jnp.where(query_pos >= end, end, first)
        visible = (key_pos >= first) & (key_pos <= query_pos)
        hide_ref[n] = jnp.where(visible, 0.0, HIDDEN)

    hide(0, seg)
    if shipped:
        hide(1, from_seg)

    factor = math.log2(math.e) / math.sqrt(head_dim)

    def att_copy(unit):
        return pltpu.make_async_remote_copy(
            src_ref=sent_ref.at[unit],
            dst_ref=got_ref.at[unit],
            send_sem=att_send.at[unit],
            recv_sem=att_recv.at[unit],
            device_id={"segment": to_seg},
            device_id_type=MESH,
        )

    def receive(h):
        if relayed(h):

            @pl.when(ctx == 3)
            def _():
                kv_send(2, h).wait_recv()
                relay(h).start()

        for by in range(back, 0, -1):
            known = ctx >= by
            if relayed(h) and by == 2:
                known = ctx == 2

            @pl.when(known)
            def _():
                kv_send(by, h).wait_recv()

    def attend(h, hidden, ref):
        blocks = [seen_ref.at[h, by - 1] for by in range(back, 0, -1)] + [kv_ref.at[h]]
        keys = jnp.concatenate([block[:, :head_dim] for block in blocks], axis=0)
        values = jnp.concatenate([block[:, head_dim:] for block in blocks], axis=0)
        for low in range(0, group, CHUNK):
            high = min(group, low + CHUNK)
            many = high - low
            queries = q_ref[h * group + low : h * group + high].reshape(
                many * rows, head_dim
            )
            scores = lax.dot_general(
                queries,
                keys,
                (((1,), (1,)), ((), ())),
                preferred_element_type=jnp.float32,
            )
            scores = (
                scores.reshape(many, rows, depth) + hide_ref[hidden][None]
            ).reshape(many * rows, depth)
            peak = jnp.max(scores, axis=1, keepdims=True)
            weights = jnp.exp2((scores - peak) * factor)
            denom = jnp.sum(weights, axis=1, keepdims=True)
            mixed = jnp.dot(
                weights.astype(jnp.bfloat16), values, preferred_element_type=jnp.float32
            )
            ref[h * group + low : h * group + high] = (
                (mixed * (1.0 / denom)).astype(jnp.bfloat16).reshape(many, rows, head_dim)
            )

    def arrived(h):
        if h < own:
            for g in range(group):
                att_copy(h * group + g).wait_recv()

    def total_of(n, begin, size):
        at = pl.ds(pl.multiple_of(begin, size), size)
        h = early[n]
        mixed = jnp.concatenate([got_ref[h * group + g] for g in range(group)], axis=1)
        product = jnp.dot(
            mixed,
            w_ref[pl.ds(n * width, width), at],
            preferred_element_type=jnp.float32,
        )
        return product if h == order[0] else acc_ref[:, at] + product

    def project(h):
        n = early.index(h)

        def one(k, carry):
            begin = pl.multiple_of(k * columns, columns)
            acc_ref[:, pl.ds(begin, columns)] = total_of(n, begin, columns)
            return carry

        lax.fori_loop(0, n_tp, one, 0)

    for h in range(own):
        receive(h)
        attend(h, 0, sent_ref)
        for g in range(group):
            att_copy(h * group + g).start()
        if shipped and h == 0:
            ship(0).wait_recv()
            spread(own)
    if shipped:
        receive(own)
        ship(1).wait_recv()
        attend(own, 1, got_ref)

    order = [h for h in early if h >= own] + [h for h in early if h < own]

    def share_copy(by, n):
        at = pl.ds(n * tile, tile)
        return pltpu.make_async_remote_copy(
            src_ref=part_ref.at[by - 1, :, at],
            dst_ref=share_ref.at[by - 1, :, at],
            send_sem=share_send.at[by - 1, n],
            recv_sem=share_recv.at[by - 1, n],
            device_id={"tp": lax.rem(tp + by, n_tp)},
            device_id_type=MESH,
        )

    def forward(by, g):
        return pltpu.make_async_remote_copy(
            src_ref=got_ref.at[last * group + g],
            dst_ref=peer_got.at[by - 1, g],
            send_sem=fwd_send.at[by - 1, g],
            recv_sem=fwd_recv.at[by - 1, g],
            device_id={"tp": lax.rem(tp + by, n_tp)},
            device_id_type=MESH,
        )

    def hand_on(g):
        att_copy(last * group + g).wait_recv()
        for by in range(1, n_tp):
            forward(by, g).start()

    handed = 0
    for h in order:
        arrived(h)
        w_copy(early.index(h)).wait()
        if h != order[-1]:
            project(h)
            continue
        for by in range(1, n_tp):
            peer = lax.rem(tp + by, n_tp)
            for n in range(tiles):
                part_ref[by - 1, :, pl.ds(n * tile, tile)] = total_of(
                    early.index(h), peer * columns + n * tile, tile
                ).astype(jnp.bfloat16)
                share_copy(by, n).start()
        handed = handed + 1
        hand_on(0)
        begin = pl.multiple_of(tp * columns, columns)
        acc_ref[:, pl.ds(begin, columns)] = total_of(
            early.index(h), begin, columns
        )

    def finish(g):
        own_w_copy(g).wait()
        for by in range(1, n_tp):
            peer_w_copy(by, g).wait_recv()
            forward(by, g).wait_recv()
        mixed = jnp.concatenate(
            [got_ref[last * group + g]] + [peer_got[by - 1, g] for by in range(1, n_tp)],
            axis=1,
        )
        into = pl.ds(pl.multiple_of(tp * columns, columns), columns)
        total = jnp.dot(mixed, last_w[g], preferred_element_type=jnp.float32)
        if order or g > 0:
            total = total + acc_ref[:, into]
        if g < group - 1:
            acc_ref[:, into] = total
            return
        if order:
            for by in range(1, n_tp):
                for n in range(tiles):
                    share_copy(by, n).wait_recv()
                total = total + share_ref[by - 1].astype(jnp.float32)
        out_ref[...] = total.astype(jnp.bfloat16)

    for g in range(group):
        if g >= handed:
            hand_on(g)
        if g > 0:
            finish(g - 1)
    finish(group - 1)

    for unit in range(own * group):
        att_copy(unit).wait_send()
    for h in range(heads):
        for by in range(1, back + 1):

            @pl.when(sends_to(ctx, by, h))
            def _():
                kv_send(by, h).wait_send()

        if relayed(h):

            @pl.when(ctx == 3)
            def _():
                relay(h).wait_send()

    if shipped:
        for n in range(2):
            ship(n).wait_send()
    for by in range(1, n_tp):
        for g in range(group):
            peer_w_copy(by, g).wait_send()
            forward(by, g).wait_send()
        if order:
            for n in range(tiles):
                share_copy(by, n).wait_send()


CHUNK = 5


def local(n_seg, n_ctx, n_tp, queries, pairs, out_proj, lengths):
    rows, heads = pairs.shape[1], pairs.shape[2]
    head_dim = pairs.shape[3] // 2
    width = queries.shape[3]
    group = width // head_dim
    model = out_proj.shape[3]
    columns = model // n_tp
    back = min(n_ctx - 1, -(-(rows * n_ctx // 2 - 1) // rows))
    tiles = columns // tile_of(columns)
    shipped = 1 if heads > 1 else 0
    own = heads - shipped
    sizes = (n_seg, n_ctx, n_tp, rows, heads, head_dim, group, back, shipped)
    bf16, f32 = jnp.bfloat16, jnp.float32
    dma = pltpu.SemaphoreType.DMA
    anywhere = pl.BlockSpec(memory_space=pl.ANY)

    def flat(array, parts):
        array = with_layout_constraint(
            array.reshape(rows, heads, parts, head_dim),
            Layout(major_to_minor=(0, 2, 1, 3)),
        )
        return array.transpose(0, 2, 1, 3).reshape(rows * parts * heads, head_dim)

    result = pl.pallas_call(
        functools.partial(kernel, sizes),
        out_shape=jax.ShapeDtypeStruct((rows, columns), bf16),
        in_specs=[anywhere] * 4,
        out_specs=pl.BlockSpec(memory_space=pltpu.VMEM),
        scratch_shapes=[
            pltpu.SMEM(lengths.shape, jnp.int32),
            pltpu.VMEM((rows * group * heads, head_dim), bf16),
            pltpu.VMEM((rows * 2 * heads, head_dim), bf16),
            pltpu.VMEM((rows * group * heads, head_dim), f32),
            pltpu.VMEM((rows * 2 * heads, head_dim), f32),
            pltpu.VMEM((heads * group, rows, head_dim), bf16),
            pltpu.VMEM((heads, rows, 2 * head_dim), bf16),
            pltpu.VMEM((group, rows, head_dim), bf16),
            pltpu.VMEM((rows, 2 * head_dim), bf16),
            pltpu.VMEM((max(1, heads - 1) * width, model), bf16),
            pltpu.VMEM((group, n_tp * head_dim, columns), bf16),
            pltpu.VMEM((heads, back, rows, 2 * head_dim), bf16),
            pltpu.VMEM((1 + shipped, rows, (back + 1) * rows), f32),
            pltpu.VMEM((own * group, rows, head_dim), bf16),
            pltpu.VMEM((heads * group, rows, head_dim), bf16),
            pltpu.VMEM((n_tp - 1, group, rows, head_dim), bf16),
            pltpu.VMEM((rows, model), f32),
            pltpu.VMEM((n_tp - 1, rows, columns), bf16),
            pltpu.VMEM((n_tp - 1, rows, columns), bf16),
            dma,
            dma((2,)),
            dma((max(1, heads - 1),)),
            dma((group,)),
            dma((n_tp - 1, group)),
            dma((n_tp - 1, group)),
            dma((2,)),
            dma((2,)),
            dma((back, heads)),
            dma((back, heads)),
            dma((own * group,)),
            dma((own * group,)),
            dma((n_tp - 1, group)),
            dma((n_tp - 1, group)),
            dma((n_tp - 1, tiles)),
            dma((n_tp - 1, tiles)),
        ],
        compiler_params=pltpu.CompilerParams(
            collective_id=0, has_side_effects=True, vmem_limit_bytes=44 << 20
        ),
    )(
        pltpu.with_memory_space_constraint(lengths, pltpu.HBM),
        pltpu.with_memory_space_constraint(flat(queries, group), pltpu.HBM),
        pltpu.with_memory_space_constraint(flat(pairs, 2), pltpu.HBM),
        out_proj.reshape(heads * width, model),
    )
    return result.reshape(1, rows, columns)


def solution(mesh):
    sizes = [mesh.shape[axis] for axis in ("segment", "ctx", "tp")]
    return jax.shard_map(
        functools.partial(local, *sizes),
        mesh=mesh,
        in_specs=(
            P("segment", "ctx", "tp", None),
            P("segment", "ctx", "tp", None),
            P("segment", "tp", None, None),
            P(),
        ),
        out_specs=P("segment", "ctx", "tp"),
        check_vma=False,
    )
```

```python
import functools
import math

import jax
import jax.numpy as jnp
from jax import lax
from jax.experimental import pallas as pl
from jax.experimental.layout import Layout, with_layout_constraint
from jax.experimental.pallas import tpu as pltpu
from jax.sharding import PartitionSpec as P

MESH = pl.DeviceIdType.MESH
HIDDEN = -1e30


def tile_of(columns):
    for tile in (1280, 640, 512, 256, 128):
        if columns % tile == 0:
            return tile
    return columns


def kernel(
    sizes,
    lengths_hbm,
    q_hbm,
    kv_hbm,
    w_hbm,
    out_ref,
    lengths_ref,
    q_raw,
    kv_raw,
    q_wide,
    kv_wide,
    q_ref,
    kv_ref,
    ship_q,
    ship_kv,
    w_ref,
    last_w,
    seen_ref,
    hide_ref,
    sent_ref,
    got_ref,
    peer_got,
    acc_ref,
    part_ref,
    share_ref,
    lengths_sem,
    raw_sem,
    w_sem,
    own_w_sem,
    peer_w_send,
    peer_w_recv,
    ship_send,
    ship_recv,
    seen_send,
    seen_recv,
    att_send,
    att_recv,
    fwd_send,
    fwd_recv,
    share_send,
    share_recv,
):
    n_seg, n_ctx, n_tp, rows, heads, head_dim, group, back, shipped = sizes
    seg = lax.axis_index("segment")
    ctx = lax.axis_index("ctx")
    tp = lax.axis_index("tp")
    width = group * head_dim
    columns = out_ref.shape[1]
    tile = tile_of(columns)
    tiles = columns // tile
    depth = (back + 1) * rows
    own = heads - shipped
    last = own - 1
    early = [h for h in range(heads) if h != last]
    order = [h for h in early if h >= own] + [h for h in early if h < own]
    to_seg = lax.rem(seg + n_seg - 1, n_seg)
    from_seg = lax.rem(seg + 1, n_seg)
    relays = n_ctx == 4 and back == 2

    def relayed(h):
        return relays and h > 0

    lengths_copy = pltpu.make_async_copy(lengths_hbm, lengths_ref, lengths_sem)
    kv_copy = pltpu.make_async_copy(kv_hbm, kv_raw, raw_sem.at[0])
    q_copy = pltpu.make_async_copy(q_hbm, q_raw, raw_sem.at[1])
    kv_copy.start()
    q_copy.start()
    lengths_copy.start()

    barrier = pltpu.get_barrier_semaphore()

    def sends_to(source, by, h=0):
        there = (source >= 0) & (source + by < n_ctx)
        return there & (source != 1) if relayed(h) and by == 1 else there

    awaited = jnp.int32(1 + n_tp - 1)
    pl.semaphore_signal(
        barrier, inc=1, device_id={"segment": from_seg}, device_id_type=MESH
    )
    for by in range(1, back + 1):
        awaited = awaited + sends_to(ctx, by).astype(jnp.int32)

        @pl.when(sends_to(ctx - by, by))
        def _():
            pl.semaphore_signal(
                barrier, inc=1, device_id={"ctx": ctx - by}, device_id_type=MESH
            )

    if relays:
        awaited = awaited + (ctx == 3).astype(jnp.int32)

        @pl.when(ctx == 2)
        def _():
            pl.semaphore_signal(
                barrier, inc=1, device_id={"ctx": 3}, device_id_type=MESH
            )

    for by in range(1, n_tp):
        pl.semaphore_signal(
            barrier,
            inc=1,
            device_id={"tp": lax.rem(tp + by, n_tp)},
            device_id_type=MESH,
        )

    def w_copy(n):
        return pltpu.make_async_copy(
            w_hbm.at[pl.ds(early[n] * width, width)],
            w_ref.at[pl.ds(n * width, width)],
            w_sem.at[n],
        )

    def own_w_copy(g):
        return pltpu.make_async_copy(
            w_hbm.at[
                pl.ds(last * width + g * head_dim, head_dim),
                pl.ds(pl.multiple_of(tp * columns, columns), columns),
            ],
            last_w.at[g, pl.ds(0, head_dim)],
            own_w_sem.at[g],
        )

    def peer_w_copy(by, g):
        peer = lax.rem(tp + by, n_tp)
        return pltpu.make_async_remote_copy(
            src_ref=w_hbm.at[
                pl.ds(last * width + g * head_dim, head_dim),
                pl.ds(pl.multiple_of(peer * columns, columns), columns),
            ],
            dst_ref=last_w.at[g, pl.ds(by * head_dim, head_dim)],
            send_sem=peer_w_send.at[by - 1, g],
            recv_sem=peer_w_recv.at[by - 1, g],
            device_id={"tp": peer},
            device_id_type=MESH,
        )

    def split_kv(h, ref):
        for part in range(2):
            ref[:, part * head_dim : (part + 1) * head_dim] = kv_wide[
                pl.ds(part * heads + h, rows, stride=2 * heads), :
            ].astype(jnp.bfloat16)

    def split_q(h, ref, base):
        for g in range(group):
            ref[base + g] = q_wide[
                pl.ds(g * heads + h, rows, stride=group * heads), :
            ].astype(jnp.bfloat16)

    kv_copy.wait()
    kv_wide[...] = kv_raw[...].astype(jnp.float32)
    for h in range(own):
        split_kv(h, kv_ref.at[h])
    if shipped:
        split_kv(own, ship_kv)
    q_copy.wait()
    q_wide[...] = q_raw[...].astype(jnp.float32)
    for n in [early.index(h) for h in order]:
        w_copy(n).start()
    for g in range(group):
        own_w_copy(g).start()
    if shipped:
        split_q(own, ship_q, 0)

    pl.semaphore_wait(barrier, awaited)

    def ship(n):
        return pltpu.make_async_remote_copy(
            src_ref=(ship_kv, ship_q)[n],
            dst_ref=(kv_ref.at[own], q_ref.at[pl.ds(own * group, group)])[n],
            send_sem=ship_send.at[n],
            recv_sem=ship_recv.at[n],
            device_id={"segment": to_seg},
            device_id_type=MESH,
        )

    def kv_send(by, h):
        return pltpu.make_async_remote_copy(
            src_ref=kv_ref.at[h],
            dst_ref=seen_ref.at[h, by - 1],
            send_sem=seen_send.at[by - 1, h],
            recv_sem=seen_recv.at[by - 1, h],
            device_id={"ctx": lax.rem(ctx + by, n_ctx)},
            device_id_type=MESH,
        )

    def relay(h):
        return pltpu.make_async_remote_copy(
            src_ref=seen_ref.at[h, 1],
            dst_ref=seen_ref.at[h, 0],
            send_sem=seen_send.at[0, h],
            recv_sem=seen_recv.at[0, h],
            device_id={"ctx": 2},
            device_id_type=MESH,
        )

    def spread(h):
        for by in range(back, 0, -1):

            @pl.when(sends_to(ctx, by, h))
            def _():
                kv_send(by, h).start()

    if shipped:
        for n in range(2):
            ship(n).start()
    for h in range(own):
        spread(h)
    for g in range(group):
        for by in range(1, n_tp):
            peer_w_copy(by, g).start()

    for by in range(1, back + 1):

        @pl.when(ctx < by)
        def _():
            for h in range(heads):
                seen_ref[h, by - 1] = jnp.zeros((rows, 2 * head_dim), seen_ref.dtype)

    for h in range(own):
        split_q(h, q_ref, h * group)

    lengths_copy.wait()
    query_pos = ctx * rows + lax.broadcasted_iota(jnp.int32, (rows, depth), 0)
    key_pos = (ctx - back) * rows + lax.broadcasted_iota(jnp.int32, (rows, depth), 1)

    def hide(n, batch):
        first = jnp.zeros((rows, depth), jnp.int32)
        end = jnp.int32(0)
        for k in range(lengths_ref.shape[1]):
            end = end + lengths_ref[batch, k]
            first = jnp.where(query_pos >= end, end, first)
        visible = (key_pos >= first) & (key_pos <= query_pos)
        hide_ref[n] = jnp.where(visible, 0.0, HIDDEN)

    hide(0, seg)
    if shipped:
        hide(1, from_seg)

    factor = math.log2(math.e) / math.sqrt(head_dim)

    def att_copy(unit):
        return pltpu.make_async_remote_copy(
            src_ref=sent_ref.at[unit],
            dst_ref=got_ref.at[unit],
            send_sem=att_send.at[unit],
            recv_sem=att_recv.at[unit],
            device_id={"segment": to_seg},
            device_id_type=MESH,
        )

    def receive(h):
        if relayed(h):

            @pl.when(ctx == 3)
            def _():
                kv_send(2, h).wait_recv()
                relay(h).start()

        for by in range(back, 0, -1):
            known = ctx >= by
            if relayed(h) and by == 2:
                known = ctx == 2

            @pl.when(known)
            def _():
                kv_send(by, h).wait_recv()

    def attend(h, hidden, ref):
        blocks = [seen_ref.at[h, by - 1] for by in range(back, 0, -1)] + [kv_ref.at[h]]
        keys = jnp.concatenate([block[:, :head_dim] for block in blocks], axis=0)
        values = jnp.concatenate([block[:, head_dim:] for block in blocks], axis=0)
        for low in range(0, group, CHUNK):
            high = min(group, low + CHUNK)
            many = high - low
            queries = q_ref[h * group + low : h * group + high].reshape(
                many * rows, head_dim
            )
            scores = lax.dot_general(
                queries,
                keys,
                (((1,), (1,)), ((), ())),
                preferred_element_type=jnp.float32,
            )
            scores = (
                scores.reshape(many, rows, depth) + hide_ref[hidden][None]
            ).reshape(many * rows, depth)
            peak = jnp.max(scores, axis=1, keepdims=True)
            weights = jnp.exp2((scores - peak) * factor)
            denom = jnp.sum(weights, axis=1, keepdims=True)
            mixed = jnp.dot(
                weights.astype(jnp.bfloat16), values, preferred_element_type=jnp.float32
            )
            ref[h * group + low : h * group + high] = (
                (mixed * (1.0 / denom)).astype(jnp.bfloat16).reshape(many, rows, head_dim)
            )

    def arrived(h):
        if h < own:
            for g in range(group):
                att_copy(h * group + g).wait_recv()

    def total_of(n, begin, size):
        at = pl.ds(pl.multiple_of(begin, size), size)
        h = early[n]
        mixed = jnp.concatenate([got_ref[h * group + g] for g in range(group)], axis=1)
        product = jnp.dot(
            mixed,
            w_ref[pl.ds(n * width, width), at],
            preferred_element_type=jnp.float32,
        )
        return product if h == order[0] else acc_ref[:, at] + product

    def project(h):
        n = early.index(h)

        def one(k, carry):
            begin = pl.multiple_of(k * columns, columns)
            acc_ref[:, pl.ds(begin, columns)] = total_of(n, begin, columns)
            return carry

        lax.fori_loop(0, n_tp, one, 0)

    for h in range(own):
        receive(h)
        attend(h, 0, sent_ref)
        for g in range(group):
            att_copy(h * group + g).start()
        if shipped and h == 0:
            ship(0).wait_recv()
            spread(own)
    if shipped:
        receive(own)
        ship(1).wait_recv()
        attend(own, 1, got_ref)


    def share_copy(by, n):
        at = pl.ds(n * tile, tile)
        return pltpu.make_async_remote_copy(
            src_ref=part_ref.at[by - 1, :, at],
            dst_ref=share_ref.at[by - 1, :, at],
            send_sem=share_send.at[by - 1, n],
            recv_sem=share_recv.at[by - 1, n],
            device_id={"tp": lax.rem(tp + by, n_tp)},
            device_id_type=MESH,
        )

    def forward(by, g):
        return pltpu.make_async_remote_copy(
            src_ref=got_ref.at[last * group + g],
            dst_ref=peer_got.at[by - 1, g],
            send_sem=fwd_send.at[by - 1, g],
            recv_sem=fwd_recv.at[by - 1, g],
            device_id={"tp": lax.rem(tp + by, n_tp)},
            device_id_type=MESH,
        )

    def hand_on(g):
        att_copy(last * group + g).wait_recv()
        for by in range(1, n_tp):
            forward(by, g).start()

    handed = 0
    for h in order:
        arrived(h)
        w_copy(early.index(h)).wait()
        if h != order[-1]:
            project(h)
            continue
        for by in range(1, n_tp):
            peer = lax.rem(tp + by, n_tp)
            for n in range(tiles):
                part_ref[by - 1, :, pl.ds(n * tile, tile)] = total_of(
                    early.index(h), peer * columns + n * tile, tile
                ).astype(jnp.bfloat16)
                share_copy(by, n).start()
        handed = handed + 1
        hand_on(0)
        begin = pl.multiple_of(tp * columns, columns)
        acc_ref[:, pl.ds(begin, columns)] = total_of(
            early.index(h), begin, columns
        )

    def finish(g):
        own_w_copy(g).wait()
        for by in range(1, n_tp):
            peer_w_copy(by, g).wait_recv()
            forward(by, g).wait_recv()
        mixed = jnp.concatenate(
            [got_ref[last * group + g]] + [peer_got[by - 1, g] for by in range(1, n_tp)],
            axis=1,
        )
        into = pl.ds(pl.multiple_of(tp * columns, columns), columns)
        total = jnp.dot(mixed, last_w[g], preferred_element_type=jnp.float32)
        if order or g > 0:
            total = total + acc_ref[:, into]
        if g < group - 1:
            acc_ref[:, into] = total
            return
        if order:
            for by in range(1, n_tp):
                for n in range(tiles):
                    share_copy(by, n).wait_recv()
                total = total + share_ref[by - 1].astype(jnp.float32)
        out_ref[...] = total.astype(jnp.bfloat16)

    for g in range(handed, min(group, 3)):
        hand_on(g)
    for g in range(group):
        finish(g)
        if g + 3 < group:
            hand_on(g + 3)

    for unit in range(own * group):
        att_copy(unit).wait_send()
    for h in range(heads):
        for by in range(1, back + 1):

            @pl.when(sends_to(ctx, by, h))
            def _():
                kv_send(by, h).wait_send()

        if relayed(h):

            @pl.when(ctx == 3)
            def _():
                relay(h).wait_send()

    if shipped:
        for n in range(2):
            ship(n).wait_send()
    for by in range(1, n_tp):
        for g in range(group):
            peer_w_copy(by, g).wait_send()
            forward(by, g).wait_send()
        if order:
            for n in range(tiles):
                share_copy(by, n).wait_send()


CHUNK = 5


def local(n_seg, n_ctx, n_tp, queries, pairs, out_proj, lengths):
    rows, heads = pairs.shape[1], pairs.shape[2]
    head_dim = pairs.shape[3] // 2
    width = queries.shape[3]
    group = width // head_dim
    model = out_proj.shape[3]
    columns = model // n_tp
    back = min(n_ctx - 1, -(-(rows * n_ctx // 2 - 1) // rows))
    tiles = columns // tile_of(columns)
    shipped = 1 if heads > 1 else 0
    own = heads - shipped
    sizes = (n_seg, n_ctx, n_tp, rows, heads, head_dim, group, back, shipped)
    bf16, f32 = jnp.bfloat16, jnp.float32
    dma = pltpu.SemaphoreType.DMA
    anywhere = pl.BlockSpec(memory_space=pl.ANY)

    def flat(array, parts):
        array = with_layout_constraint(
            array.reshape(rows, heads, parts, head_dim),
            Layout(major_to_minor=(0, 2, 1, 3)),
        )
        return array.transpose(0, 2, 1, 3).reshape(rows * parts * heads, head_dim)

    result = pl.pallas_call(
        functools.partial(kernel, sizes),
        out_shape=jax.ShapeDtypeStruct((rows, columns), bf16),
        in_specs=[anywhere] * 4,
        out_specs=pl.BlockSpec(memory_space=pltpu.VMEM),
        scratch_shapes=[
            pltpu.SMEM(lengths.shape, jnp.int32),
            pltpu.VMEM((rows * group * heads, head_dim), bf16),
            pltpu.VMEM((rows * 2 * heads, head_dim), bf16),
            pltpu.VMEM((rows * group * heads, head_dim), f32),
            pltpu.VMEM((rows * 2 * heads, head_dim), f32),
            pltpu.VMEM((heads * group, rows, head_dim), bf16),
            pltpu.VMEM((heads, rows, 2 * head_dim), bf16),
            pltpu.VMEM((group, rows, head_dim), bf16),
            pltpu.VMEM((rows, 2 * head_dim), bf16),
            pltpu.VMEM((max(1, heads - 1) * width, model), bf16),
            pltpu.VMEM((group, n_tp * head_dim, columns), bf16),
            pltpu.VMEM((heads, back, rows, 2 * head_dim), bf16),
            pltpu.VMEM((1 + shipped, rows, (back + 1) * rows), f32),
            pltpu.VMEM((own * group, rows, head_dim), bf16),
            pltpu.VMEM((heads * group, rows, head_dim), bf16),
            pltpu.VMEM((n_tp - 1, group, rows, head_dim), bf16),
            pltpu.VMEM((rows, model), f32),
            pltpu.VMEM((n_tp - 1, rows, columns), bf16),
            pltpu.VMEM((n_tp - 1, rows, columns), bf16),
            dma,
            dma((2,)),
            dma((max(1, heads - 1),)),
            dma((group,)),
            dma((n_tp - 1, group)),
            dma((n_tp - 1, group)),
            dma((2,)),
            dma((2,)),
            dma((back, heads)),
            dma((back, heads)),
            dma((own * group,)),
            dma((own * group,)),
            dma((n_tp - 1, group)),
            dma((n_tp - 1, group)),
            dma((n_tp - 1, tiles)),
            dma((n_tp - 1, tiles)),
        ],
        compiler_params=pltpu.CompilerParams(
            collective_id=0, has_side_effects=True, vmem_limit_bytes=44 << 20
        ),
    )(
        pltpu.with_memory_space_constraint(lengths, pltpu.HBM),
        pltpu.with_memory_space_constraint(flat(queries, group), pltpu.HBM),
        pltpu.with_memory_space_constraint(flat(pairs, 2), pltpu.HBM),
        out_proj.reshape(heads * width, model),
    )
    return result.reshape(1, rows, columns)


def solution(mesh):
    sizes = [mesh.shape[axis] for axis in ("segment", "ctx", "tp")]
    return jax.shard_map(
        functools.partial(local, *sizes),
        mesh=mesh,
        in_specs=(
            P("segment", "ctx", "tp", None),
            P("segment", "ctx", "tp", None),
            P("segment", "tp", None, None),
            P(),
        ),
        out_specs=P("segment", "ctx", "tp"),
        check_vma=False,
    )
```

```python
import functools
import math

import jax
import jax.numpy as jnp
from jax import lax
from jax.experimental import pallas as pl
from jax.experimental.layout import Layout, with_layout_constraint
from jax.experimental.pallas import tpu as pltpu
from jax.sharding import PartitionSpec as P

MESH = pl.DeviceIdType.MESH
HIDDEN = -1e30


def tile_of(columns):
    for tile in (512, 256, 128):
        if columns % tile == 0:
            return tile
    return columns


def kernel(
    sizes,
    lengths_hbm,
    q_hbm,
    kv_hbm,
    w_hbm,
    out_ref,
    lengths_ref,
    q_raw,
    kv_raw,
    q_wide,
    kv_wide,
    q_ref,
    kv_ref,
    ship_q,
    ship_kv,
    w_ref,
    last_w,
    seen_ref,
    hide_ref,
    sent_ref,
    got_ref,
    peer_got,
    acc_ref,
    part_ref,
    share_ref,
    lengths_sem,
    raw_sem,
    w_sem,
    own_w_sem,
    peer_w_send,
    peer_w_recv,
    ship_send,
    ship_recv,
    seen_send,
    seen_recv,
    att_send,
    att_recv,
    fwd_send,
    fwd_recv,
    share_send,
    share_recv,
):
    n_seg, n_ctx, n_tp, rows, heads, head_dim, group, back, shipped = sizes
    seg = lax.axis_index("segment")
    ctx = lax.axis_index("ctx")
    tp = lax.axis_index("tp")
    width = group * head_dim
    columns = out_ref.shape[1]
    tile = tile_of(columns)
    tiles = columns // tile
    depth = (back + 1) * rows
    own = heads - shipped
    late = own - min(own, 2)
    units = (own - late) * group
    early = [h for h in range(heads) if not late <= h < own]
    order = [h for h in early if h >= own] + [h for h in early if h < own]
    to_seg = lax.rem(seg + n_seg - 1, n_seg)
    from_seg = lax.rem(seg + 1, n_seg)
    relays = n_ctx == 4 and back == 2

    def relayed(h):
        return relays and h > 0

    lengths_copy = pltpu.make_async_copy(lengths_hbm, lengths_ref, lengths_sem)
    kv_copy = pltpu.make_async_copy(kv_hbm, kv_raw, raw_sem.at[0])
    q_copy = pltpu.make_async_copy(q_hbm, q_raw, raw_sem.at[1])
    kv_copy.start()
    q_copy.start()
    lengths_copy.start()

    barrier = pltpu.get_barrier_semaphore()

    def sends_to(source, by, h=0):
        there = (source >= 0) & (source + by < n_ctx)
        return there & (source != 1) if relayed(h) and by == 1 else there

    awaited = jnp.int32(1 + n_tp - 1)
    pl.semaphore_signal(
        barrier, inc=1, device_id={"segment": from_seg}, device_id_type=MESH
    )
    for by in range(1, back + 1):
        awaited = awaited + sends_to(ctx, by).astype(jnp.int32)

        @pl.when(sends_to(ctx - by, by))
        def _():
            pl.semaphore_signal(
                barrier, inc=1, device_id={"ctx": ctx - by}, device_id_type=MESH
            )

    if relays:
        awaited = awaited + (ctx == 3).astype(jnp.int32)

        @pl.when(ctx == 2)
        def _():
            pl.semaphore_signal(
                barrier, inc=1, device_id={"ctx": 3}, device_id_type=MESH
            )

    for by in range(1, n_tp):
        pl.semaphore_signal(
            barrier,
            inc=1,
            device_id={"tp": lax.rem(tp + by, n_tp)},
            device_id_type=MESH,
        )

    def w_copy(n):
        return pltpu.make_async_copy(
            w_hbm.at[pl.ds(early[n] * width, width)],
            w_ref.at[pl.ds(n * width, width)],
            w_sem.at[n],
        )

    def own_w_copy(g):
        return pltpu.make_async_copy(
            w_hbm.at[
                pl.ds(late * width + g * head_dim, head_dim),
                pl.ds(pl.multiple_of(tp * columns, columns), columns),
            ],
            last_w.at[g, pl.ds(0, head_dim)],
            own_w_sem.at[g],
        )

    def peer_w_copy(by, g):
        peer = lax.rem(tp + by, n_tp)
        return pltpu.make_async_remote_copy(
            src_ref=w_hbm.at[
                pl.ds(late * width + g * head_dim, head_dim),
                pl.ds(pl.multiple_of(peer * columns, columns), columns),
            ],
            dst_ref=last_w.at[g, pl.ds(by * head_dim, head_dim)],
            send_sem=peer_w_send.at[by - 1, g],
            recv_sem=peer_w_recv.at[by - 1, g],
            device_id={"tp": peer},
            device_id_type=MESH,
        )

    def split_kv(h, ref):
        for part in range(2):
            ref[:, part * head_dim : (part + 1) * head_dim] = kv_wide[
                pl.ds(part * heads + h, rows, stride=2 * heads), :
            ].astype(jnp.bfloat16)

    def split_q(h, ref, base):
        for g in range(group):
            ref[base + g] = q_wide[
                pl.ds(g * heads + h, rows, stride=group * heads), :
            ].astype(jnp.bfloat16)

    kv_copy.wait()
    kv_wide[...] = kv_raw[...].astype(jnp.float32)
    for h in range(own):
        split_kv(h, kv_ref.at[h])
    if shipped:
        split_kv(own, ship_kv)
    q_copy.wait()
    q_wide[...] = q_raw[...].astype(jnp.float32)
    for n in [early.index(h) for h in order]:
        w_copy(n).start()
    for g in range(units):
        own_w_copy(g).start()
    if shipped:
        split_q(own, ship_q, 0)

    pl.semaphore_wait(barrier, awaited)

    def ship(n):
        return pltpu.make_async_remote_copy(
            src_ref=(ship_kv, ship_q)[n],
            dst_ref=(kv_ref.at[own], q_ref.at[pl.ds(own * group, group)])[n],
            send_sem=ship_send.at[n],
            recv_sem=ship_recv.at[n],
            device_id={"segment": to_seg},
            device_id_type=MESH,
        )

    def kv_send(by, h):
        return pltpu.make_async_remote_copy(
            src_ref=kv_ref.at[h],
            dst_ref=seen_ref.at[h, by - 1],
            send_sem=seen_send.at[by - 1, h],
            recv_sem=seen_recv.at[by - 1, h],
            device_id={"ctx": lax.rem(ctx + by, n_ctx)},
            device_id_type=MESH,
        )

    def relay(h):
        return pltpu.make_async_remote_copy(
            src_ref=seen_ref.at[h, 1],
            dst_ref=seen_ref.at[h, 0],
            send_sem=seen_send.at[0, h],
            recv_sem=seen_recv.at[0, h],
            device_id={"ctx": 2},
            device_id_type=MESH,
        )

    def spread(h):
        for by in range(back, 0, -1):

            @pl.when(sends_to(ctx, by, h))
            def _():
                kv_send(by, h).start()

    if shipped:
        for n in range(2):
            ship(n).start()
    for h in range(own):
        spread(h)
    for g in range(units):
        for by in range(1, n_tp):
            peer_w_copy(by, g).start()

    for by in range(1, back + 1):

        @pl.when(ctx < by)
        def _():
            for h in range(heads):
                seen_ref[h, by - 1] = jnp.zeros((rows, 2 * head_dim), seen_ref.dtype)

    for h in range(own):
        split_q(h, q_ref, h * group)

    lengths_copy.wait()
    query_pos = ctx * rows + lax.broadcasted_iota(jnp.int32, (rows, depth), 0)
    key_pos = (ctx - back) * rows + lax.broadcasted_iota(jnp.int32, (rows, depth), 1)

    def hide(n, batch):
        first = jnp.zeros((rows, depth), jnp.int32)
        end = jnp.int32(0)
        for k in range(lengths_ref.shape[1]):
            end = end + lengths_ref[batch, k]
            first = jnp.where(query_pos >= end, end, first)
        visible = (key_pos >= first) & (key_pos <= query_pos)
        hide_ref[n] = jnp.where(visible, 0.0, HIDDEN)

    hide(0, seg)
    if shipped:
        hide(1, from_seg)

    factor = math.log2(math.e) / math.sqrt(head_dim)

    def att_copy(unit):
        return pltpu.make_async_remote_copy(
            src_ref=sent_ref.at[unit],
            dst_ref=got_ref.at[unit],
            send_sem=att_send.at[unit],
            recv_sem=att_recv.at[unit],
            device_id={"segment": to_seg},
            device_id_type=MESH,
        )

    def pass_on(h):
        if relayed(h):

            @pl.when(ctx == 3)
            def _():
                kv_send(2, h).wait_recv()
                relay(h).start()

    def receive(h):
        for by in range(back, 0, -1):
            known = ctx >= by
            if relayed(h) and by == 2:
                known = ctx == 2

            @pl.when(known)
            def _():
                kv_send(by, h).wait_recv()

    def attend(h, hidden, ref):
        blocks = [seen_ref.at[h, by - 1] for by in range(back, 0, -1)] + [kv_ref.at[h]]
        keys = jnp.concatenate([block[:, :head_dim] for block in blocks], axis=0)
        values = jnp.concatenate([block[:, head_dim:] for block in blocks], axis=0)
        for low in range(0, group, CHUNK):
            high = min(group, low + CHUNK)
            many = high - low
            queries = q_ref[h * group + low : h * group + high].reshape(
                many * rows, head_dim
            )
            scores = lax.dot_general(
                queries,
                keys,
                (((1,), (1,)), ((), ())),
                preferred_element_type=jnp.float32,
            )
            scores = (
                scores.reshape(many, rows, depth) + hide_ref[hidden][None]
            ).reshape(many * rows, depth)
            peak = jnp.max(scores, axis=1, keepdims=True)
            weights = jnp.exp2((scores - peak) * factor)
            denom = jnp.sum(weights, axis=1, keepdims=True)
            mixed = jnp.dot(
                weights.astype(jnp.bfloat16), values, preferred_element_type=jnp.float32
            )
            ref[h * group + low : h * group + high] = (
                (mixed * (1.0 / denom)).astype(jnp.bfloat16).reshape(many, rows, head_dim)
            )

    def arrived(h):
        if h < own:
            for g in range(group):
                att_copy(h * group + g).wait_recv()

    def total_of(n, begin, size):
        at = pl.ds(pl.multiple_of(begin, size), size)
        h = early[n]
        mixed = jnp.concatenate([got_ref[h * group + g] for g in range(group)], axis=1)
        product = jnp.dot(
            mixed,
            w_ref[pl.ds(n * width, width), at],
            preferred_element_type=jnp.float32,
        )
        return product if h == order[0] else acc_ref[:, at] + product

    def project(h):
        n = early.index(h)

        def one(k, carry):
            begin = pl.multiple_of(k * columns, columns)
            acc_ref[:, pl.ds(begin, columns)] = total_of(n, begin, columns)
            return carry

        lax.fori_loop(0, n_tp, one, 0)

    for h in range(own):
        receive(h)
        attend(h, 0, sent_ref)
        for g in range(group):
            att_copy(h * group + g).start()
        if h + 1 < heads:
            pass_on(h + 1)
        if shipped and h == 0:
            ship(0).wait_recv()
            spread(own)
    if shipped:
        receive(own)
        ship(1).wait_recv()
        attend(own, 1, got_ref)


    def share_copy(by, n):
        at = pl.ds(n * tile, tile)
        return pltpu.make_async_remote_copy(
            src_ref=part_ref.at[by - 1, :, at],
            dst_ref=share_ref.at[by - 1, :, at],
            send_sem=share_send.at[by - 1, n],
            recv_sem=share_recv.at[by - 1, n],
            device_id={"tp": lax.rem(tp + by, n_tp)},
            device_id_type=MESH,
        )

    def forward(by, g):
        return pltpu.make_async_remote_copy(
            src_ref=got_ref.at[late * group + g],
            dst_ref=peer_got.at[by - 1, g],
            send_sem=fwd_send.at[by - 1, g],
            recv_sem=fwd_recv.at[by - 1, g],
            device_id={"tp": lax.rem(tp + by, n_tp)},
            device_id_type=MESH,
        )

    def hand_on(g):
        att_copy(late * group + g).wait_recv()
        for by in range(1, n_tp):
            forward(by, g).start()

    for h in order:
        arrived(h)
        w_copy(early.index(h)).wait()
        if h != order[-1]:
            project(h)
            continue
        for by in range(1, n_tp):
            peer = lax.rem(tp + by, n_tp)
            part_ref[by - 1] = total_of(
                early.index(h), peer * columns, columns
            ).astype(jnp.bfloat16)
        for g in range(min(units, 2)):
            hand_on(g)
        begin = pl.multiple_of(tp * columns, columns)
        acc_ref[:, pl.ds(begin, columns)] = total_of(
            early.index(h), begin, columns
        )

    def finish(g):
        own_w_copy(g).wait()
        for by in range(1, n_tp):
            peer_w_copy(by, g).wait_recv()
            forward(by, g).wait_recv()
        mixed = jnp.concatenate(
            [got_ref[late * group + g]] + [peer_got[by - 1, g] for by in range(1, n_tp)],
            axis=1,
        )
        into = pl.ds(pl.multiple_of(tp * columns, columns), columns)
        total = jnp.dot(mixed, last_w[g], preferred_element_type=jnp.float32)
        if order or g > 0:
            total = total + acc_ref[:, into]
        if order and g == sum_at:
            for by in range(1, n_tp):
                for n in range(tiles):
                    share_copy(by, n).wait_recv()
                total = total + share_ref[by - 1].astype(jnp.float32)
        if g < units - 1:
            acc_ref[:, into] = total
            return
        out_ref[...] = total.astype(jnp.bfloat16)

    sum_at = max(0, units - 3)
    handed = min(units, 2) if order else 0
    for g in range(units):
        for ahead in range(handed, min(units, g + 4)):
            hand_on(ahead)
        handed = max(handed, min(units, g + 4))
        if order:
            for n in range(tiles):
                if min(n, sum_at) == g:
                    for by in range(1, n_tp):
                        share_copy(by, n).start()
        finish(g)

    for unit in range(own * group):
        att_copy(unit).wait_send()
    for h in range(heads):
        for by in range(1, back + 1):

            @pl.when(sends_to(ctx, by, h))
            def _():
                kv_send(by, h).wait_send()

        if relayed(h):

            @pl.when(ctx == 3)
            def _():
                relay(h).wait_send()

    if shipped:
        for n in range(2):
            ship(n).wait_send()
    for by in range(1, n_tp):
        for g in range(units):
            peer_w_copy(by, g).wait_send()
            forward(by, g).wait_send()
        if order:
            for n in range(tiles):
                share_copy(by, n).wait_send()


CHUNK = 5


def local(n_seg, n_ctx, n_tp, queries, pairs, out_proj, lengths):
    rows, heads = pairs.shape[1], pairs.shape[2]
    head_dim = pairs.shape[3] // 2
    width = queries.shape[3]
    group = width // head_dim
    model = out_proj.shape[3]
    columns = model // n_tp
    back = min(n_ctx - 1, -(-(rows * n_ctx // 2 - 1) // rows))
    tiles = columns // tile_of(columns)
    shipped = 1 if heads > 1 else 0
    own = heads - shipped
    units = min(own, 2) * group
    kept = max(1, heads - min(own, 2))
    sizes = (n_seg, n_ctx, n_tp, rows, heads, head_dim, group, back, shipped)
    bf16, f32 = jnp.bfloat16, jnp.float32
    dma = pltpu.SemaphoreType.DMA
    anywhere = pl.BlockSpec(memory_space=pl.ANY)

    def flat(array, parts):
        array = with_layout_constraint(
            array.reshape(rows, heads, parts, head_dim),
            Layout(major_to_minor=(0, 2, 1, 3)),
        )
        return array.transpose(0, 2, 1, 3).reshape(rows * parts * heads, head_dim)

    result = pl.pallas_call(
        functools.partial(kernel, sizes),
        out_shape=jax.ShapeDtypeStruct((rows, columns), bf16),
        in_specs=[anywhere] * 4,
        out_specs=pl.BlockSpec(memory_space=pltpu.VMEM),
        scratch_shapes=[
            pltpu.SMEM(lengths.shape, jnp.int32),
            pltpu.VMEM((rows * group * heads, head_dim), bf16),
            pltpu.VMEM((rows * 2 * heads, head_dim), bf16),
            pltpu.VMEM((rows * group * heads, head_dim), f32),
            pltpu.VMEM((rows * 2 * heads, head_dim), f32),
            pltpu.VMEM((heads * group, rows, head_dim), bf16),
            pltpu.VMEM((heads, rows, 2 * head_dim), bf16),
            pltpu.VMEM((group, rows, head_dim), bf16),
            pltpu.VMEM((rows, 2 * head_dim), bf16),
            pltpu.VMEM((kept * width, model), bf16),
            pltpu.VMEM((units, n_tp * head_dim, columns), bf16),
            pltpu.VMEM((heads, back, rows, 2 * head_dim), bf16),
            pltpu.VMEM((1 + shipped, rows, (back + 1) * rows), f32),
            pltpu.VMEM((own * group, rows, head_dim), bf16),
            pltpu.VMEM((heads * group, rows, head_dim), bf16),
            pltpu.VMEM((n_tp - 1, units, rows, head_dim), bf16),
            pltpu.VMEM((rows, model), f32),
            pltpu.VMEM((n_tp - 1, rows, columns), bf16),
            pltpu.VMEM((n_tp - 1, rows, columns), bf16),
            dma,
            dma((2,)),
            dma((kept,)),
            dma((units,)),
            dma((n_tp - 1, units)),
            dma((n_tp - 1, units)),
            dma((2,)),
            dma((2,)),
            dma((back, heads)),
            dma((back, heads)),
            dma((own * group,)),
            dma((own * group,)),
            dma((n_tp - 1, units)),
            dma((n_tp - 1, units)),
            dma((n_tp - 1, tiles)),
            dma((n_tp - 1, tiles)),
        ],
        compiler_params=pltpu.CompilerParams(
            collective_id=0, has_side_effects=True, vmem_limit_bytes=48 << 20
        ),
    )(
        pltpu.with_memory_space_constraint(lengths, pltpu.HBM),
        pltpu.with_memory_space_constraint(flat(queries, group), pltpu.HBM),
        pltpu.with_memory_space_constraint(flat(pairs, 2), pltpu.HBM),
        out_proj.reshape(heads * width, model),
    )
    return result.reshape(1, rows, columns)


def solution(mesh):
    sizes = [mesh.shape[axis] for axis in ("segment", "ctx", "tp")]
    return jax.shard_map(
        functools.partial(local, *sizes),
        mesh=mesh,
        in_specs=(
            P("segment", "ctx", "tp", None),
            P("segment", "ctx", "tp", None),
            P("segment", "tp", None, None),
            P(),
        ),
        out_specs=P("segment", "ctx", "tp"),
        check_vma=False,
    )
```
